32 devices in a mesh: groups: 2 (over x), depth: 16 (over z, y, core).
Axes of the slice: x: 2, y: 2, z: 4, core: 2. Of those that a mesh axis runs over, the one named last changes fastest.
Arguments:
- voxels: bfloat16 [256, 32, 16384], P(('groups', 'depth')), parts along dimension 0, may hold values from -6 to 6
- offsets: int32 [256], P('groups'), parts along dimension 0, may hold values from 0 to 127
- w_first: bfloat16 [64, 32], replicated, may hold values from -1 to 1
- decoder_second_weight: bfloat16 [33, 64], replicated, may hold values from -0.75 to 0.75
- cotangent: float32 [32, 32768], P(None, ('groups', 'depth')), parts along dimension 1, may hold values from -6 to 6
Outputs:
- image: float32 [32, 32768], P(None, ('groups', 'depth')), parts along dimension 1
- grad_voxels: bfloat16 [256, 32, 16384], P(('groups', 'depth')), parts along dimension 0
- grad_first: float32 [128, 32], P('groups'), parts along dimension 0
- grad_second: float32 [66, 64], P('groups'), parts along dimension 0
The draws below stay inside these ranges and needn't reach their ends.
There are 2 independent parts, one for each index of `groups`. The reference program is written for one: setup_inputs(seed, part) draws one part's arguments, and reference() takes and returns one part's arrays. A program takes and returns all parts, laid end to end along the dimension named above; an argument that names none is the same for every part. Nothing has to cross between parts.
Inputs may be any that keep to these rules, and one draw needn't show every extreme that they name: offsets[p] counts tiles of 128 rays.
All inputs are finite; a program needn't handle non-finite values.
Results may differ from the reference program's by a relative error of at most 0.0085.
Values may be sent and summed in bfloat16 or wider, within the bound.
A program may use at most 192 MiB of HBM per device.

```python
import jax
import jax.numpy as jnp
from jax import lax

F = 32
H = 64
C = 32
TILE = 128
RAYS = 16384
NPL = 128


def plant(result, own_key, smallest, top_value):
    extent = result.shape
    place = [jax.random.randint(jax.random.fold_in(own_key, axis), (), 0, extent[axis]) for axis in range(len(extent))]
    result = result.at[tuple(place)].set(smallest)
    longest = extent.index(max(extent))
    place[longest] = (place[longest] + 1) % extent[longest]
    return result.at[tuple(place)].set(top_value)


def shard_levels(rng, shape, shards, smallest, high):
    level, own = 1.0, jax.random.fold_in(rng, 6)
    for dim, shards_of in shards:
        heights = jnp.exp(jax.random.uniform(jax.random.fold_in(own, dim), (shards_of,), jnp.float32, smallest / len(shards), high / len(shards)))
        level = level * jnp.repeat(heights, shape[dim] // shards_of).reshape([-1 if axis == dim else 1 for axis in range(len(shape))])
    return level


def normal_values(own_key, extent, spread, limit, shards=(), dtype=jnp.bfloat16):
    result = spread * jax.random.normal(own_key, extent, jnp.float32)
    if shards:
        result = result * shard_levels(own_key, extent, shards, -0.22, 0.18)
    return jnp.clip(result, -limit, limit).astype(dtype)


def setup_inputs(seed: int = 0, part: int = 0) -> dict:
    key_of = jax.random.split(jax.random.key(seed), 6)
    part_splits = jax.random.split(jax.random.fold_in(key_of[5], part), 6)
    return {
        "voxels": normal_values(part_splits[0], (NPL, F, RAYS), 1.0, 6.0, ((0, 16),)),
        "offsets": plant(jax.random.randint(part_splits[1], (NPL,), 0, RAYS // TILE), jax.random.fold_in(part_splits[1], 1), 0, (RAYS // TILE) - 1).astype(jnp.int32),
        "w_first": normal_values(key_of[2], (H, F), F ** -0.5, 1.0),
        "decoder_second_weight": normal_values(key_of[3], (C + 1, H), H ** -0.5, 0.75),
        "cotangent": normal_values(part_splits[4], (C, RAYS), 1.0, 6.0, ((1, 16),), jnp.float32),
    }


def decode_plane(plane, w_first, decoder_second_weight):
    preact = jnp.dot(w_first, plane, preferred_element_type=jnp.float32)
    hidden = jax.nn.silu(preact).astype(jnp.bfloat16)
    output_raw = jnp.dot(decoder_second_weight, hidden, preferred_element_type=jnp.float32)
    return preact, hidden, output_raw


def make_slab(output_raw, dscale):
    channels = output_raw.shape[0] - 1
    emitted_light = jax.nn.sigmoid(output_raw[:channels])
    density = jax.nn.softplus(output_raw[channels]) * dscale
    return jnp.concatenate([emitted_light, density[None]], 0).astype(jnp.bfloat16)


def move_rays(values, start):
    doubled = jnp.concatenate([values, values], values.ndim - 1)
    return lax.dynamic_slice_in_dim(doubled, start.astype(jnp.int32), values.shape[-1], values.ndim - 1)


def blended_image(slabs, upstream_gradient):
    channels = slabs.shape[1] - 1
    emitted_light = slabs[:, :channels].astype(jnp.float32)
    density = slabs[:, channels].astype(jnp.float32)
    passing = jnp.exp(-density)
    through = jnp.cumprod(passing, axis=0)
    before = jnp.concatenate([jnp.ones_like(through[:1]), through[:-1]], 0)
    sample_weight_rows = before * (1.0 - passing)
    pixel_colour = jnp.einsum("vi,vsi->si", sample_weight_rows, emitted_light)
    objective_value = jnp.einsum("vz,dvz->dz", upstream_gradient, emitted_light)
    running = jnp.cumsum(sample_weight_rows * objective_value, axis=0)
    return passing, before, sample_weight_rows, objective_value, running, through[-1], pixel_colour


def slab_gradient(passing, before, sample_weight_rows, objective_value, running, upstream_gradient, enter, prior, ray_total):
    grad_rad = (enter * sample_weight_rows)[:, None, :] * upstream_gradient[None]
    grad_dens = enter * before * passing * objective_value - (ray_total - (prior + enter * running))
    return jnp.concatenate([grad_rad, grad_dens[:, None, :]], 1).astype(jnp.bfloat16)


def plane_backward(carry, inputs, w_first, decoder_second_weight, dscale):
    plane, grad_sheared, shift_tiles = inputs
    rays_count = plane.shape[1]
    preact, hidden, output_raw = decode_plane(plane, w_first, decoder_second_weight)
    grad_slab = move_rays(grad_sheared, rays_count - TILE * shift_tiles).astype(jnp.float32)
    channels = output_raw.shape[0] - 1
    sig_rad = jax.nn.sigmoid(output_raw[:channels])
    grad_rad = grad_slab[:channels] * sig_rad * (1.0 - sig_rad)
    grad_dens = grad_slab[channels] * dscale * jax.nn.sigmoid(output_raw[channels])
    grad_raw = jnp.concatenate([grad_rad, grad_dens[None]], 0).astype(jnp.bfloat16)
    grad_hidden = jnp.dot(decoder_second_weight.T, grad_raw, preferred_element_type=jnp.float32)
    sig_pre = jax.nn.sigmoid(preact)
    grad_pre = (grad_hidden * sig_pre * (1.0 + preact * (1.0 - sig_pre))).astype(jnp.bfloat16)
    grad_plane = jnp.dot(w_first.T, grad_pre, preferred_element_type=jnp.float32).astype(jnp.bfloat16)
    contract = (((1,), (1,)), ((), ()))
    acc_first = carry[0] + lax.dot_general(grad_pre, plane, contract, preferred_element_type=jnp.float32)
    acc_second = carry[1] + lax.dot_general(grad_raw, hidden, contract, preferred_element_type=jnp.float32)
    return (acc_first, acc_second), grad_plane


def reference(voxels, offsets, w_first, decoder_second_weight, cotangent):
    dscale = 3.0 / NPL

    def forward_plane(inputs):
        plane, shift_tiles = inputs
        output_raw = decode_plane(plane, w_first, decoder_second_weight)[2]
        return move_rays(make_slab(output_raw, dscale), TILE * shift_tiles)

    slabs = lax.map(forward_plane, (voxels, offsets))
    passing, before, sample_weight_rows, objective_value, running, last_pass, image = blended_image(slabs, cotangent)
    ray_total = jnp.sum(cotangent * image, axis=0)
    grad_sheared = slab_gradient(passing, before, sample_weight_rows, objective_value, running, cotangent, 1.0, 0.0, ray_total)

    def step_plane(carry, inputs):
        return plane_backward(carry, inputs, w_first, decoder_second_weight, dscale)

    start = (jnp.zeros(w_first.shape, jnp.float32), jnp.zeros(decoder_second_weight.shape, jnp.float32))
    grads, grad_voxels = lax.scan(step_plane, start, (voxels, grad_sheared, offsets))
    return image, grad_voxels, grads[0], grads[1]
```

```python
import functools

import jax
import jax.numpy as jnp
from jax import lax
from jax.experimental import pallas as pl
from jax.experimental.pallas import tpu as pltpu
from jax.sharding import PartitionSpec as P

TILE = 128
PACK = 4
FSUB = 256
BSUB = 256
GSUB = 512
LIMIT = 191 * 2**18
BF = jnp.bfloat16
F32 = jnp.float32
NT = (((1,), (1,)), ((), ()))


def dot(a, b):
    return jnp.dot(a, b, preferred_element_type=F32)


def running_sum(x):
    rows = x.shape[0]
    row = lax.broadcasted_iota(jnp.int32, x.shape, 0)
    s = 1
    while s < rows:
        x = x + jnp.where(row >= s, pltpu.roll(x, s, 0), 0.0)
        s *= 2
    return x


def wrap(t, total):
    if total & (total - 1) == 0:
        return t & (total - 1)
    return lax.rem(t, total)


def first_tile(off_ref, planes, p):
    return off_ref[lax.axis_index("depth") * planes + p]


def tile_at(base, j, rays):
    return pl.ds(pl.multiple_of(wrap(base + j, rays // TILE) * TILE, TILE), TILE)


def absorb(dens):
    upto = running_sum(dens)
    passing = jnp.exp(-dens)
    before = jnp.exp(dens - upto)
    return upto, passing, before


def softplus(x):
    return jnp.maximum(x, 0.0) + jnp.log1p(jnp.exp(-jnp.abs(x)))


def picks(shape, period, dim):
    other = lax.broadcasted_iota(jnp.int32, shape, 1 - dim)
    return (lax.rem(lax.broadcasted_iota(jnp.int32, shape, dim), period) == other).astype(BF)


def diagonal(shape, rows, cols):
    r = lax.broadcasted_iota(jnp.int32, shape, 0) // rows
    return r == lax.broadcasted_iota(jnp.int32, shape, 1) // cols


def repeat_blocks(w):
    rows, cols = w.shape
    tall = dot(picks((PACK * rows, rows), rows, 0), w).astype(BF)
    full = dot(tall, picks((cols, PACK * cols), cols, 1))
    return jnp.where(diagonal(full.shape, rows, cols), full, 0.0)


def prepare(first_ref, second_ref, w1_ref, w1t_ref, w2_ref, w2t_ref):
    planes = PACK * w2_ref.shape[0]
    chans, hid = second_ref.shape[0] - 1, second_ref.shape[1]
    w1t = repeat_blocks(first_ref[...])
    w1t_ref[...] = w1t.astype(BF)
    w1_ref[...] = (0.5 * w1t).T.astype(BF)
    rad = repeat_blocks(second_ref[0:chans, :])
    dens = dot(second_ref[chans : chans + 1, :], picks((hid, PACK * hid), hid, 1))
    dens = jnp.broadcast_to(dens, (planes, PACK * hid))
    block = lax.broadcasted_iota(jnp.int32, dens.shape, 1) // hid
    plane = lax.broadcasted_iota(jnp.int32, dens.shape, 0)
    for h in range(planes // PACK):
        mine = jnp.where(plane == block + h * PACK, dens, 0.0)
        w2_ref[h] = jnp.concatenate([0.5 * rad, mine], 0).astype(BF)
        w2t_ref[h] = (0.5 * jnp.concatenate([rad, mine], 0)).T.astype(BF)


def remote(src, dst, send_sem, recv_sem, to):
    return pltpu.make_async_remote_copy(
        src_ref=src,
        dst_ref=dst,
        send_sem=send_sem,
        recv_sem=recv_sem,
        device_id={"depth": to},
        device_id_type=pl.DeviceIdType.MESH,
    )


def turn(i, n):
    if n & (n - 1):
        return i
    c, bit = 0, 1
    while bit < n:
        c = c + ((i // bit) % 2) * (n // (2 * bit))
        bit *= 2
    return c


def each(n, body):
    def step(d, carry):
        body(d)
        return carry

    lax.fori_loop(0, n, step, 0)


def fused_kernel(
    dscale,
    xs,
    first_ref,
    second_ref,
    cot_ref,
    image_ref,
    gsh,
    g1_ref,
    g2_ref,
    hids,
    slope,
    srad,
    wgt,
    bpass,
    dsig,
    graw,
    w1,
    w1t,
    w2,
    w2t,
    acc1,
    acc2,
    cots,
    csend,
    crecv,
    tsend,
    trecv,
    back,
    land,
    held,
    give,
    got,
    mine,
    full,
    sem_c,
    rem_c,
    sem_t,
    rem_t,
    sem_b,
    rem_b,
    sem_k,
    rem_k,
    sem_r,
    s1,
    r1,
    s2,
    r2,
):
    n, chans, width = cots.shape
    halves, rows = w2.shape[0], w2.shape[1]
    planes = PACK * halves
    feats = xs.shape[1] // planes
    kin, kmid = w1.shape[1], w1.shape[0]
    wide = rows - planes
    lag = n // 2
    me = lax.axis_index("depth")
    chip, core = me // 2, me % 2
    partner = me + 1 - 2 * core

    barrier = pltpu.get_barrier_semaphore()
    for s in range(1, n):
        pl.semaphore_signal(
            barrier,
            inc=1,
            device_id={"depth": (me + s) % n},
            device_id_type=pl.DeviceIdType.MESH,
        )
    cots[me] = cot_ref[...].astype(BF)
    acc1[...] = jnp.zeros_like(acc1)
    acc2[...] = jnp.zeros_like(acc2)
    prepare(first_ref, second_ref, w1, w1t, w2, w2t)
    pl.semaphore_wait(barrier, n - 1)

    def colour_copy(c):
        return remote(csend.at[c], crecv.at[me], sem_c.at[c], rem_c.at[me], c)

    def colour_here(d):
        return remote(csend.at[d], crecv.at[d], sem_c.at[d], rem_c.at[d], d)

    def through_copy(c):
        return remote(tsend.at[c], trecv.at[me], sem_t.at[c], rem_t.at[me], c)

    def through_here(d):
        return remote(tsend.at[d], trecv.at[d], sem_t.at[d], rem_t.at[d], d)

    def reply_copy(d):
        return remote(back.at[d], land.at[me], sem_b.at[d], rem_b.at[me], d)

    def reply_here(c):
        return remote(back.at[c], land.at[c], sem_b.at[c], rem_b.at[c], c)

    def cot_copy(s):
        to = partner if s == 0 else (me + 2 * s) % n
        return remote(cots.at[me], cots.at[me], sem_k.at[s], rem_k.at[me], to)

    def relay_copy(c):
        return remote(cots.at[c], cots.at[c], sem_r.at[c], rem_k.at[c], partner)

    def hand_on(c):
        @pl.when(c != me)
        def _():
            colour_copy(c).start()
            through_copy(c).start()

        @pl.when(c == me)
        def _():
            crecv[me] = csend[me]
            trecv[me] = tsend[me]

    def relays(c):
        return jnp.logical_and(c % 2 == core, c != me)

    def settle():
        def arrived(d):
            @pl.when(d != me)
            def _():
                colour_here(d).wait_recv()
                through_here(d).wait_recv()

        each(n, arrived)
        cot = cot_ref[...]

        row = lax.broadcasted_iota(jnp.int32, held.shape, 0)
        held[...] = (row == 0).astype(F32)
        image_ref[...] = jnp.zeros_like(image_ref)

        def fold(d):
            enter = held[0:1, :]
            prior = held[1:2, :]
            colour = crecv[d].astype(F32)
            back[d, 0:1, :] = enter
            back[d, 1:2, :] = prior
            held[2:3, :] = trecv[d]
            image_ref[...] += enter * colour
            held[1:2, :] = prior + enter * jnp.sum(cot * colour, axis=0, keepdims=True)
            held[0:1, :] = enter * held[2:3, :]

        each(n, fold)
        total = held[1:2, :]

        def turn_round(d):
            back[d, 1:2, :] = total - back[d, 1:2, :]

        each(n, turn_round)

        def answer(d):
            @pl.when(d != me)
            def _():
                reply_copy(d).start()

        each(n, answer)
        land[me] = back[me]

    def later(c):
        @pl.when(relays(c))
        def _():
            relay_copy(c).wait_recv()
            relay_copy(c).start()

        @pl.when(c == me)
        def _():
            settle()

    fsub = min(FSUB, width)

    def forward(i, carry):
        c = turn(i, n)

        @pl.when(i > 0)
        def _():
            hand_on(turn(i - 1, n))

        @pl.when(c == me)
        def _():
            for s in range(n // 2):
                cot_copy(s).start()

        @pl.when(i >= lag)
        def _():
            later(turn(i - lag, n))

        for b in range(width // fsub):
            here = pl.ds(b * fsub, fsub)
            raw_d = None
            for h in range(halves):
                x = xs[c, pl.ds(h * kin, kin), here]
                half = dot(w1[...], x)
                t = jnp.tanh(half)
                up = 1.0 + t
                hidden = half * up
                slope[c, pl.ds(h * kmid, kmid), here] = (up + hidden * (1.0 - t)).astype(BF)
                hidden = hidden.astype(BF)
                hids[c, pl.ds(h * kmid, kmid), here] = hidden
                out = dot(w2[h], hidden)
                srad[c, pl.ds(h * wide, wide), here] = jnp.tanh(out[:wide]).astype(BF)
                d = out[wide:]
                raw_d = d if raw_d is None else raw_d + d
            dens = softplus(raw_d) * dscale
            upto, passing, before = absorb(dens)
            weight = before * (1.0 - passing)
            wgt[c, :, here] = weight
            bpass[c, :, here] = before * passing
            dsig[c, :, here] = dscale * (0.5 * jnp.tanh(0.5 * raw_d) + 0.5)
            weight = 0.5 * weight
            colour = jnp.sum(weight, axis=0, keepdims=True)
            for p in range(planes):
                s = srad[c, pl.ds(p * chans, chans), here].astype(F32)
                colour = colour + weight[p : p + 1] * s
            csend[c, :, here] = colour.astype(BF)
            tsend[c, :, here] = jnp.exp(-upto[planes - 1 : planes])
        return carry

    lax.fori_loop(0, n, forward, 0)

    ones = diagonal((planes, planes * chans), 1, chans).astype(BF)
    bsub = min(BSUB, width)

    def backward(i, carry):
        c = turn(i, n)

        @pl.when(i == 0)
        def _():
            hand_on(turn(n - 1, n))

        @pl.when(i < n - lag)
        def _():
            later(turn(i + lag, n))

        @pl.when(c % 2 != core)
        def _():
            relay_copy(c).wait_recv()

        @pl.when(c != me)
        def _():
            reply_here(c).wait_recv()

        for b in range(width // bsub):
            here = pl.ds(b * bsub, bsub)
            cot = cots[c, :, here]
            prod = jnp.concatenate(
                [cot * srad[c, pl.ds(p * chans, chans), here] for p in range(planes)], 0
            )
            score = 0.5 * (jnp.sum(cot.astype(F32), axis=0, keepdims=True) + dot(ones, prod))
            enter = land[c, 0:1, here]
            rest = land[c, 1:2, here]
            weight = enter * wgt[c, :, here]
            running = running_sum(weight * score)
            grad_d = enter * bpass[c, :, here] * score - (rest - running)
            grad_d = (grad_d * dsig[c, :, here]).astype(BF)
            weight = 0.25 * weight
            for h in range(halves):
                for k in range(PACK):
                    p = h * PACK + k
                    s = srad[c, pl.ds(p * chans, chans), here]
                    w = jnp.broadcast_to(weight[p : p + 1], (chans, bsub)).astype(BF)
                    graw[h, pl.ds(k * chans, chans), here] = (w * cot) * (1.0 - s * s)
                graw[h, pl.ds(wide, planes), here] = grad_d
                ghid = dot(w2t[h], graw[h, :, here]).astype(BF)
                mid = pl.ds(h * kmid, kmid)
                slope[c, mid, here] = ghid * slope[c, mid, here]
        for h in range(halves):
            mid = pl.ds(h * kmid, kmid)
            acc1[...] += lax.dot_general(
                slope[c, mid, :], xs[c, pl.ds(h * kin, kin), :], NT, preferred_element_type=F32
            )
            acc2[h] += lax.dot_general(graw[h], hids[c, mid, :], NT, preferred_element_type=F32)
        return carry

    lax.fori_loop(0, n, backward, 0)

    fold_grads(n, acc1, acc2, feats, chans, give)
    copies = swap(n, me, lambda to: give.at[to], got, s1, r1)
    got[me] = give[me]

    gsub = min(GSUB, width)

    def voxel_grads(c, carry):
        for b in range(width // gsub):
            here = pl.ds(b * gsub, gsub)
            for h in range(halves):
                gx = dot(w1t[...], slope[c, pl.ds(h * kmid, kmid), here])
                gsh[c, pl.ds(h * kin, kin), here] = gx.astype(BF)
        return carry

    lax.fori_loop(0, n // 2, voxel_grads, 0)
    for copy in copies:
        copy.wait()
    mine[...] = jnp.sum(got[...], axis=0)
    copies = swap(n, me, lambda to: mine, full, s2, r2)
    full[me] = mine[...]
    lax.fori_loop(n // 2, n, voxel_grads, 0)
    for copy in copies:
        copy.wait()
    both = jnp.concatenate([full[d] for d in range(n)], 0)
    g2_ref[...] = both[: chans + 1, : both.shape[0]]
    square = jnp.concatenate([both, jnp.zeros_like(both)], 0).T
    g1_ref[...] = square[both.shape[0] : both.shape[0] + feats, : both.shape[0]]

    def finish(d):
        @pl.when(d != me)
        def _():
            colour_copy(d).wait_send()
            through_copy(d).wait_send()
            reply_copy(d).wait_send()

        @pl.when(relays(d))
        def _():
            relay_copy(d).wait_send()

    each(n, finish)
    for s in range(n // 2):
        cot_copy(s).wait_send()


def swap(n, me, source, target, send_sem, recv_sem):
    copies = []
    for s in range(1, n):
        to = lax.rem(me + s, n)
        copies.append(remote(source(to), target.at[me], send_sem.at[s], recv_sem.at[s], to))
    for copy in copies:
        copy.start()
    return copies


def fold_grads(n, a1_ref, a2_ref, feats, chans, give):
    hid = a1_ref.shape[0] // PACK
    halves, rows = a2_ref.shape[0], a2_ref.shape[1]
    part = give.shape[1]

    def aligned(ref_rows, k, size):
        at = k * size
        lane = at % TILE
        piece = ref_rows[:, at - lane : at - lane + TILE]
        return pltpu.roll(piece, TILE - lane, 1) if lane else piece

    g1 = g2 = gd = None
    for k in range(PACK):
        one = aligned(a1_ref[pl.ds(k * hid, hid), :], k, feats)
        g1 = one if g1 is None else g1 + one
    for h in range(halves):
        tail = a2_ref[h, pl.ds(PACK * chans, rows - PACK * chans), :]
        row = lax.broadcasted_iota(jnp.int32, (tail.shape[0], TILE), 0)
        for k in range(PACK):
            two = aligned(a2_ref[h, pl.ds(k * chans, chans), :], k, hid)
            g2 = two if g2 is None else g2 + two
            dens = jnp.where(row == h * PACK + k, aligned(tail, k, hid), 0.0)
            dens = jnp.sum(dens, axis=0, keepdims=True)
            gd = dens if gd is None else gd + dens
    lanes = lax.broadcasted_iota(jnp.int32, (hid, TILE), 1)
    rest = hid - chans - 1
    low = jnp.concatenate([g2, gd, jnp.zeros((rest, TILE), F32)], 0)
    both = jnp.where(lanes < hid, low, pltpu.roll(g1, hid, 1))
    for d in range(n):
        give[d] = both[d * part : (d + 1) * part]


def moves(off_ref, planes, feats, n, width, rays, pair):
    me = lax.axis_index("depth")
    tiles, per = rays // TILE, width // TILE
    for p in range(planes):
        base = off_ref[me * planes + p]
        rows = pl.ds(p * feats, feats)

        def chunk(c):
            first = wrap(base + c * per, tiles)

            @pl.when(first + per <= tiles)
            def _():
                at = pl.ds(pl.multiple_of(first * TILE, TILE), width)
                pair((p, slice(None), at), (c, rows)).start()

            @pl.when(first + per > tiles)
            def _():
                for j in range(per):
                    spot = (c, rows, pl.ds(j * TILE, TILE))
                    pair((p, slice(None), tile_at(first, j, rays)), spot).start()

        each(n, chunk)


def shear_kernel(off_ref, vox_ref, x_ref, sem):
    planes, feats, rays = vox_ref.shape
    n, _, width = x_ref.shape

    def pair(plain, sheared):
        return pltpu.make_async_copy(vox_ref.at[plain], x_ref.at[sheared], sem)

    moves(off_ref, planes, feats, n, width, rays, pair)
    pltpu.make_async_copy(x_ref, x_ref, sem).wait()


def place_kernel(off_ref, gsh_ref, image_in, g1_in, g2_in, gvox_ref, image_ref, g1_ref, g2_ref, sem):
    planes, feats, rays = gvox_ref.shape
    n, _, width = gsh_ref.shape

    def pair(plain, sheared):
        return pltpu.make_async_copy(gsh_ref.at[sheared], gvox_ref.at[plain], sem)

    moves(off_ref, planes, feats, n, width, rays, pair)
    image_ref[...] = image_in[...]
    g1_ref[...] = g1_in[...]
    g2_ref[...] = g2_in[...]
    pltpu.make_async_copy(gsh_ref, gsh_ref, sem).wait()


def shards(voxels, offsets, w_first, w_second, cotangent):
    planes, feats, rays = voxels.shape
    hid = w_first.shape[0]
    chans, chunk = cotangent.shape
    n = lax.axis_size("depth")
    halves = planes // PACK
    dscale = 3.0 / (planes * n)
    rows = PACK * chans + planes

    smem = pl.BlockSpec(memory_space=pltpu.SMEM)
    vmem = pl.BlockSpec(memory_space=pltpu.VMEM)
    hbm = pl.BlockSpec(memory_space=pltpu.HBM)
    small = (
        jax.ShapeDtypeStruct((chans, chunk), F32),
        jax.ShapeDtypeStruct((feats, hid), F32),
        jax.ShapeDtypeStruct((chans + 1, hid), F32),
    )
    part = (n, hid // n, TILE)
    dma = pltpu.SemaphoreType.DMA
    chunks = pltpu.VMEM((n, planes * feats, chunk), BF)
    sheared = pl.pallas_call(
        shear_kernel,
        out_shape=chunks,
        in_specs=[smem, hbm],
        out_specs=vmem,
        scratch_shapes=[dma],
        compiler_params=pltpu.CompilerParams(vmem_limit_bytes=4 * 2**20),
        name="shear",
    )(offsets, pltpu.with_memory_space_constraint(voxels, pltpu.HBM))
    image, gsh, g1, g2 = pl.pallas_call(
        functools.partial(fused_kernel, dscale),
        out_shape=(small[0], chunks) + small[1:],
        in_specs=[vmem, vmem, vmem, vmem],
        out_specs=(vmem, vmem, vmem, vmem),
        scratch_shapes=[
            pltpu.VMEM((n, planes * hid, chunk), BF),
            pltpu.VMEM((n, planes * hid, chunk), BF),
            pltpu.VMEM((n, planes * chans, chunk), BF),
            pltpu.VMEM((n, planes, chunk), F32),
            pltpu.VMEM((n, planes, chunk), F32),
            pltpu.VMEM((n, planes, chunk), F32),
            pltpu.VMEM((halves, rows, chunk), BF),
            pltpu.VMEM((PACK * hid, PACK * feats), BF),
            pltpu.VMEM((PACK * feats, PACK * hid), BF),
            pltpu.VMEM((halves, rows, PACK * hid), BF),
            pltpu.VMEM((halves, PACK * hid, rows), BF),
            pltpu.VMEM((PACK * hid, PACK * feats), F32),
            pltpu.VMEM((halves, rows, PACK * hid), F32),
            pltpu.VMEM((n, chans, chunk), BF),
            pltpu.VMEM((n, chans, chunk), BF),
            pltpu.VMEM((n, chans, chunk), BF),
            pltpu.VMEM((n, 1, chunk), F32),
            pltpu.VMEM((n, 1, chunk), F32),
            pltpu.VMEM((n, 2, chunk), F32),
            pltpu.VMEM((n, 2, chunk), F32),
            pltpu.VMEM((8, chunk), F32),
            pltpu.VMEM(part, F32),
            pltpu.VMEM(part, F32),
            pltpu.VMEM(part[1:], F32),
            pltpu.VMEM(part, F32),
        ]
        + [dma((n,))] * 6
        + [dma((n // 2,)), dma((n,)), dma((n,))]
        + [dma((n,))] * 4,
        compiler_params=pltpu.CompilerParams(
            vmem_limit_bytes=LIMIT, collective_id=1, has_side_effects=True
        ),
        name="fused",
    )(pltpu.with_memory_space_constraint(sheared, pltpu.VMEM), w_first.T, w_second, cotangent)
    gvox, image, g1, g2 = pl.pallas_call(
        place_kernel,
        out_shape=(jax.ShapeDtypeStruct(voxels.shape, BF),) + small,
        in_specs=[smem] + [vmem] * 4,
        out_specs=(hbm, vmem, vmem, vmem),
        scratch_shapes=[dma],
        compiler_params=pltpu.CompilerParams(vmem_limit_bytes=4 * 2**20),
        name="place",
    )(offsets, pltpu.with_memory_space_constraint(gsh, pltpu.VMEM), image, g1, g2)
    return image, gvox, g1.T, g2


def solution(mesh):
    placed = (
        P(("groups", "depth"), None, None),
        P("groups"),
        P(),
        P(),
        P(None, ("groups", "depth")),
    )
    return jax.shard_map(
        shards,
        mesh=mesh,
        in_specs=placed,
        out_specs=(
            P(None, ("groups", "depth")),
            P(("groups", "depth"), None, None),
            P("groups", None),
            P("groups", None),
        ),
        check_vma=False,
    )
```

```python
import functools

import jax
import jax.numpy as jnp
from jax import lax
from jax.experimental import pallas as pl
from jax.experimental.pallas import tpu as pltpu
from jax.sharding import PartitionSpec as P

TILE = 128
PACK = 4
FSUB = 1024
BSUB = 256
GSUB = 512
CSUB = 512
LIMIT = 190 * 2**18
BF = jnp.bfloat16
F32 = jnp.float32
NT = (((1,), (1,)), ((), ()))


def dot(a, b):
    return jnp.dot(a, b, preferred_element_type=F32)


def running_sum(x):
    rows = x.shape[0]
    row = lax.broadcasted_iota(jnp.int32, x.shape, 0)
    s = 1
    while s < rows:
        x = x + jnp.where(row >= s, pltpu.roll(x, s, 0), 0.0)
        s *= 2
    return x


def wrap(t, total):
    if total & (total - 1) == 0:
        return t & (total - 1)
    return lax.rem(t, total)


def first_tile(off_ref, planes, p):
    return off_ref[lax.axis_index("depth") * planes + p]


def tile_at(base, j, rays):
    return pl.ds(pl.multiple_of(wrap(base + j, rays // TILE) * TILE, TILE), TILE)


def absorb(dens):
    upto = running_sum(dens)
    passing = jnp.exp(-dens)
    before = jnp.exp(dens - upto)
    return upto, passing, before


def softplus(x):
    return jnp.maximum(x, 0.0) + jnp.log1p(jnp.exp(-jnp.abs(x)))


def picks(shape, period, dim):
    other = lax.broadcasted_iota(jnp.int32, shape, 1 - dim)
    return (lax.rem(lax.broadcasted_iota(jnp.int32, shape, dim), period) == other).astype(BF)


def diagonal(shape, rows, cols):
    r = lax.broadcasted_iota(jnp.int32, shape, 0) // rows
    return r == lax.broadcasted_iota(jnp.int32, shape, 1) // cols


def repeat_blocks(w):
    rows, cols = w.shape
    tall = dot(picks((PACK * rows, rows), rows, 0), w).astype(BF)
    full = dot(tall, picks((cols, PACK * cols), cols, 1))
    return jnp.where(diagonal(full.shape, rows, cols), full, 0.0)


def prepare(first_ref, second_ref, w1_ref, w1t_ref, w2_ref, w2t_ref):
    planes = PACK * w2_ref.shape[0]
    chans, hid = second_ref.shape[0] - 1, second_ref.shape[1]
    w1t = repeat_blocks(first_ref[...])
    w1t_ref[...] = w1t.astype(BF)
    w1_ref[...] = (0.5 * w1t).T.astype(BF)
    rad = repeat_blocks(second_ref[0:chans, :])
    dens = dot(second_ref[chans : chans + 1, :], picks((hid, PACK * hid), hid, 1))
    dens = jnp.broadcast_to(dens, (planes, PACK * hid))
    block = lax.broadcasted_iota(jnp.int32, dens.shape, 1) // hid
    plane = lax.broadcasted_iota(jnp.int32, dens.shape, 0)
    for h in range(planes // PACK):
        mine = jnp.where(plane == block + h * PACK, dens, 0.0)
        w2_ref[h] = jnp.concatenate([0.5 * rad, mine], 0).astype(BF)
        w2t_ref[h] = (0.5 * jnp.concatenate([rad, mine], 0)).T.astype(BF)


def remote(src, dst, send_sem, recv_sem, to):
    return pltpu.make_async_remote_copy(
        src_ref=src,
        dst_ref=dst,
        send_sem=send_sem,
        recv_sem=recv_sem,
        device_id={"depth": to},
        device_id_type=pl.DeviceIdType.MESH,
    )


def turn(i, n):
    if n & (n - 1):
        return i
    c, bit = 0, 1
    while bit < n:
        c = c + ((i // bit) % 2) * (n // (2 * bit))
        bit *= 2
    return c


def each(n, body):
    def step(d, carry):
        body(d)
        return carry

    lax.fori_loop(0, n, step, 0)


def fused_kernel(
    dscale,
    xs,
    first_ref,
    second_ref,
    cot_ref,
    image_ref,
    gsh,
    g1_ref,
    g2_ref,
    hids,
    slope,
    srad,
    wgt,
    bpass,
    dsig,
    graw,
    w1,
    w1t,
    w2,
    w2t,
    acc1,
    acc2,
    cots,
    csend,
    crecv,
    tsend,
    trecv,
    back,
    land,
    held,
    raw_ref,
    give,
    got,
    mine,
    full,
    sem_c,
    rem_c,
    sem_t,
    rem_t,
    sem_b,
    rem_b,
    sem_k,
    rem_k,
    sem_r,
    s1,
    r1,
    s2,
    r2,
):
    n, chans, width = cots.shape
    halves, rows = w2.shape[0], w2.shape[1]
    planes = PACK * halves
    feats = xs.shape[1] // planes
    kin, kmid = w1.shape[1], w1.shape[0]
    wide = rows - planes
    lag = n // 2
    me = lax.axis_index("depth")
    chip, core = me // 2, me % 2
    partner = me + 1 - 2 * core

    barrier = pltpu.get_barrier_semaphore()
    for s in range(1, n):
        pl.semaphore_signal(
            barrier,
            inc=1,
            device_id={"depth": (me + s) % n},
            device_id_type=pl.DeviceIdType.MESH,
        )
    cots[me] = cot_ref[...].astype(BF)
    acc1[...] = jnp.zeros_like(acc1)
    acc2[...] = jnp.zeros_like(acc2)
    prepare(first_ref, second_ref, w1, w1t, w2, w2t)
    pl.semaphore_wait(barrier, n - 1)

    def colour_copy(c):
        return remote(csend.at[c], crecv.at[me], sem_c.at[c], rem_c.at[me], c)

    def colour_here(d):
        return remote(csend.at[d], crecv.at[d], sem_c.at[d], rem_c.at[d], d)

    def through_copy(c):
        return remote(tsend.at[c], trecv.at[me], sem_t.at[c], rem_t.at[me], c)

    def through_here(d):
        return remote(tsend.at[d], trecv.at[d], sem_t.at[d], rem_t.at[d], d)

    def reply_copy(d):
        return remote(back.at[d], land.at[me], sem_b.at[d], rem_b.at[me], d)

    def reply_here(c):
        return remote(back.at[c], land.at[c], sem_b.at[c], rem_b.at[c], c)

    def cot_copy(s):
        to = partner if s == 0 else (me + 2 * s) % n
        return remote(cots.at[me], cots.at[me], sem_k.at[s], rem_k.at[me], to)

    def relay_copy(c):
        return remote(cots.at[c], cots.at[c], sem_r.at[c], rem_k.at[c], partner)

    def hand_on(c):
        @pl.when(c != me)
        def _():
            colour_copy(c).start()
            through_copy(c).start()

        @pl.when(c == me)
        def _():
            crecv[me] = csend[me]
            trecv[me] = tsend[me]

    def relays(c):
        return jnp.logical_and(c % 2 == core, c != me)

    def settle():
        def arrived(d):
            @pl.when(d != me)
            def _():
                colour_here(d).wait_recv()
                through_here(d).wait_recv()

        each(n, arrived)
        cot = cot_ref[...]

        row = lax.broadcasted_iota(jnp.int32, held.shape, 0)
        held[...] = (row == 0).astype(F32)
        image_ref[...] = jnp.zeros_like(image_ref)

        def fold(d):
            enter = held[0:1, :]
            prior = held[1:2, :]
            colour = crecv[d].astype(F32)
            back[d, 0:1, :] = enter
            back[d, 1:2, :] = prior
            held[2:3, :] = trecv[d]
            image_ref[...] += enter * colour
            held[1:2, :] = prior + enter * jnp.sum(cot * colour, axis=0, keepdims=True)
            held[0:1, :] = enter * held[2:3, :]

        each(n, fold)
        total = held[1:2, :]

        def turn_round(d):
            back[d, 1:2, :] = total - back[d, 1:2, :]

        each(n, turn_round)

        def answer(d):
            @pl.when(d != me)
            def _():
                reply_copy(d).start()

        each(n, answer)
        land[me] = back[me]

    def later(c):
        @pl.when(relays(c))
        def _():
            relay_copy(c).wait_recv()
            relay_copy(c).start()

        @pl.when(c == me)
        def _():
            settle()

    fsub = min(FSUB, width)
    csub = min(CSUB, width)
    stack = picks((chans, planes * chans), chans, 1)

    def forward(i, carry):
        c = turn(i, n)

        @pl.when(i > 0)
        def _():
            hand_on(turn(i - 1, n))

        @pl.when(c == me)
        def _():
            for s in range(n // 2):
                cot_copy(s).start()

        @pl.when(i >= lag)
        def _():
            later(turn(i - lag, n))

        for b in range(width // fsub):
            here = pl.ds(b * fsub, fsub)
            raw_d = None
            for h in range(halves):
                mid = pl.ds(h * kmid, kmid)
                half = dot(w1[...], xs[c, pl.ds(h * kin, kin), here]).astype(BF)
                t = jnp.tanh(half)
                up = 1.0 + t
                hidden = half * up
                slope[c, mid, here] = up + hidden * (1.0 - t)
                hids[c, mid, here] = hidden
                out = dot(w2[h], hidden)
                srad[c, pl.ds(h * wide, wide), here] = jnp.tanh(out[:wide].astype(BF))
                d = out[wide:]
                raw_d = d if raw_d is None else raw_d + d
            raw_ref[:, here] = raw_d
        raw_d = raw_ref[...]
        dens = softplus(raw_d) * dscale
        upto, passing, before = absorb(dens)
        weight = before * (1.0 - passing)
        wgt[c] = weight
        bpass[c] = before * passing
        dsig[c] = dscale * (0.5 * jnp.tanh(0.5 * raw_d) + 0.5)
        weight = 0.5 * weight
        tsend[c] = jnp.exp(-upto[planes - 1 : planes])
        plain = jnp.sum(weight, axis=0, keepdims=True)
        for b in range(width // csub):
            at = slice(b * csub, (b + 1) * csub)
            here = pl.ds(b * csub, csub)
            shares = []
            for p in range(planes):
                w = jnp.broadcast_to(weight[p : p + 1, at], (chans, csub)).astype(BF)
                shares.append(w * srad[c, pl.ds(p * chans, chans), here])
            colour = plain[:, at] + dot(stack, jnp.concatenate(shares, 0))
            csend[c, :, here] = colour.astype(BF)
        return carry

    lax.fori_loop(0, n, forward, 0)

    ones = diagonal((planes, planes * chans), 1, chans).astype(BF)
    bsub = min(BSUB, width)

    def backward(i, carry):
        c = turn(i, n)

        @pl.when(i == 0)
        def _():
            hand_on(turn(n - 1, n))

        @pl.when(i < n - lag)
        def _():
            later(turn(i + lag, n))

        @pl.when(c % 2 != core)
        def _():
            relay_copy(c).wait_recv()

        @pl.when(c != me)
        def _():
            reply_here(c).wait_recv()

        for b in range(width // csub):
            here = pl.ds(b * csub, csub)
            cot = cots[c, :, here]
            prod = jnp.concatenate(
                [cot * srad[c, pl.ds(p * chans, chans), here] for p in range(planes)], 0
            )
            raw_ref[:, here] = dot(ones, prod)
        score = 0.5 * (jnp.sum(cots[c].astype(F32), axis=0, keepdims=True) + raw_ref[...])
        enter = land[c, 0:1, :]
        rest = land[c, 1:2, :]
        weight = enter * wgt[c]
        running = running_sum(weight * score)
        grad_d = enter * bpass[c] * score - (rest - running)
        grad_d = (grad_d * dsig[c]).astype(BF)
        weight = 0.25 * weight
        for h in range(halves):
            graw[h, pl.ds(wide, planes), :] = grad_d
        for b in range(width // bsub):
            at = slice(b * bsub, (b + 1) * bsub)
            here = pl.ds(b * bsub, bsub)
            cot = cots[c, :, here]
            for h in range(halves):
                for k in range(PACK):
                    p = h * PACK + k
                    s = srad[c, pl.ds(p * chans, chans), here]
                    w = jnp.broadcast_to(weight[p : p + 1, at], (chans, bsub)).astype(BF)
                    graw[h, pl.ds(k * chans, chans), here] = (w * cot) * (1.0 - s * s)
                ghid = dot(w2t[h], graw[h, :, here]).astype(BF)
                mid = pl.ds(h * kmid, kmid)
                slope[c, mid, here] = ghid * slope[c, mid, here]
        for h in range(halves):
            mid = pl.ds(h * kmid, kmid)
            acc1[...] += lax.dot_general(
                slope[c, mid, :], xs[c, pl.ds(h * kin, kin), :], NT, preferred_element_type=F32
            )
            acc2[h] += lax.dot_general(graw[h], hids[c, mid, :], NT, preferred_element_type=F32)
        return carry

    lax.fori_loop(0, n, backward, 0)

    fold_grads(n, acc1, acc2, feats, chans, give)
    copies = swap(n, me, lambda to: give.at[to], got, s1, r1)
    got[me] = give[me]

    gsub = min(GSUB, width)

    def voxel_grads(c, carry):
        for b in range(width // gsub):
            here = pl.ds(b * gsub, gsub)
            for h in range(halves):
                gx = dot(w1t[...], slope[c, pl.ds(h * kmid, kmid), here])
                gsh[c, pl.ds(h * kin, kin), here] = gx.astype(BF)
        return carry

    lax.fori_loop(0, n // 2, voxel_grads, 0)
    for copy in copies:
        copy.wait()
    mine[...] = jnp.sum(got[...], axis=0)
    copies = swap(n, me, lambda to: mine, full, s2, r2)
    full[me] = mine[...]
    lax.fori_loop(n // 2, n, voxel_grads, 0)
    for copy in copies:
        copy.wait()
    both = jnp.concatenate([full[d] for d in range(n)], 0)
    g2_ref[...] = both[: chans + 1, : both.shape[0]]
    square = jnp.concatenate([both, jnp.zeros_like(both)], 0).T
    g1_ref[...] = square[both.shape[0] : both.shape[0] + feats, : both.shape[0]]

    def finish(d):
        @pl.when(d != me)
        def _():
            colour_copy(d).wait_send()
            through_copy(d).wait_send()
            reply_copy(d).wait_send()

        @pl.when(relays(d))
        def _():
            relay_copy(d).wait_send()

    each(n, finish)
    for s in range(n // 2):
        cot_copy(s).wait_send()


def swap(n, me, source, target, send_sem, recv_sem):
    copies = []
    for s in range(1, n):
        to = lax.rem(me + s, n)
        copies.append(remote(source(to), target.at[me], send_sem.at[s], recv_sem.at[s], to))
    for copy in copies:
        copy.start()
    return copies


def whole_tiles(x):
    short = -x.shape[1] % TILE
    return jnp.concatenate([x, jnp.zeros((x.shape[0], short), x.dtype)], 1) if short else x


def fold_grads(n, a1_ref, a2_ref, feats, chans, give):
    hid = a1_ref.shape[0] // PACK
    halves, rows = a2_ref.shape[0], a2_ref.shape[1]
    part = give.shape[1]

    def aligned(ref_rows, k, size):
        at = k * size
        lane = at % TILE
        piece = ref_rows[:, at - lane : at - lane + TILE]
        return pltpu.roll(piece, TILE - lane, 1) if lane else piece

    g1 = g2 = gd = None
    for k in range(PACK):
        one = aligned(whole_tiles(a1_ref[pl.ds(k * hid, hid), :]), k, feats)
        g1 = one if g1 is None else g1 + one
    for h in range(halves):
        tail = a2_ref[h, pl.ds(PACK * chans, rows - PACK * chans), :]
        row = lax.broadcasted_iota(jnp.int32, (tail.shape[0], TILE), 0)
        for k in range(PACK):
            two = aligned(a2_ref[h, pl.ds(k * chans, chans), :], k, hid)
            g2 = two if g2 is None else g2 + two
            dens = jnp.where(row == h * PACK + k, aligned(tail, k, hid), 0.0)
            dens = jnp.sum(dens, axis=0, keepdims=True)
            gd = dens if gd is None else gd + dens
    lanes = lax.broadcasted_iota(jnp.int32, (hid, TILE), 1)
    rest = hid - chans - 1
    low = jnp.concatenate([g2, gd, jnp.zeros((rest, TILE), F32)], 0)
    both = jnp.where(lanes < hid, low, pltpu.roll(g1, hid, 1))
    for d in range(n):
        give[d] = both[d * part : (d + 1) * part]


def moves(off_ref, planes, feats, n, width, rays, pair):
    me = lax.axis_index("depth")
    tiles, per = rays // TILE, width // TILE
    for p in range(planes):
        base = off_ref[me * planes + p]
        rows = pl.ds(p * feats, feats)

        def chunk(c):
            first = wrap(base + c * per, tiles)

            @pl.when(first + per <= tiles)
            def _():
                at = pl.ds(pl.multiple_of(first * TILE, TILE), width)
                pair((p, slice(None), at), (c, rows)).start()

            @pl.when(first + per > tiles)
            def _():
                for j in range(per):
                    spot = (c, rows, pl.ds(j * TILE, TILE))
                    pair((p, slice(None), tile_at(first, j, rays)), spot).start()

        each(n, chunk)


def shear_kernel(off_ref, vox_ref, x_ref, sem):
    planes, feats, rays = vox_ref.shape
    n, _, width = x_ref.shape

    def pair(plain, sheared):
        return pltpu.make_async_copy(vox_ref.at[plain], x_ref.at[sheared], sem)

    moves(off_ref, planes, feats, n, width, rays, pair)
    pltpu.make_async_copy(x_ref, x_ref, sem).wait()


def place_kernel(off_ref, gsh_ref, image_in, g1_in, g2_in, gvox_ref, image_ref, g1_ref, g2_ref, sem):
    planes, feats, rays = gvox_ref.shape
    n, _, width = gsh_ref.shape

    def pair(plain, sheared):
        return pltpu.make_async_copy(gsh_ref.at[sheared], gvox_ref.at[plain], sem)

    moves(off_ref, planes, feats, n, width, rays, pair)
    image_ref[...] = image_in[...]
    g1_ref[...] = g1_in[...]
    g2_ref[...] = g2_in[...]
    pltpu.make_async_copy(gsh_ref, gsh_ref, sem).wait()


def shards(voxels, offsets, w_first, w_second, cotangent):
    planes, feats, rays = voxels.shape
    hid = w_first.shape[0]
    chans, chunk = cotangent.shape
    n = lax.axis_size("depth")
    halves = planes // PACK
    dscale = 3.0 / (planes * n)
    rows = PACK * chans + planes

    smem = pl.BlockSpec(memory_space=pltpu.SMEM)
    vmem = pl.BlockSpec(memory_space=pltpu.VMEM)
    hbm = pl.BlockSpec(memory_space=pltpu.HBM)
    small = (
        jax.ShapeDtypeStruct((chans, chunk), F32),
        jax.ShapeDtypeStruct((feats, hid), F32),
        jax.ShapeDtypeStruct((chans + 1, hid), F32),
    )
    held = tuple(pltpu.VMEM(a.shape, F32) for a in small)
    part = (n, hid // n, TILE)
    dma = pltpu.SemaphoreType.DMA
    chunks = pltpu.VMEM((n, planes * feats, chunk), BF)
    sheared = pl.pallas_call(
        shear_kernel,
        out_shape=chunks,
        in_specs=[smem, hbm],
        out_specs=vmem,
        scratch_shapes=[dma],
        compiler_params=pltpu.CompilerParams(vmem_limit_bytes=4 * 2**20),
        name="shear",
    )(offsets, pltpu.with_memory_space_constraint(voxels, pltpu.HBM))
    image, gsh, g1, g2 = pl.pallas_call(
        functools.partial(fused_kernel, dscale),
        out_shape=(held[0], chunks) + held[1:],
        in_specs=[vmem, vmem, vmem, vmem],
        out_specs=(vmem, vmem, vmem, vmem),
        scratch_shapes=[
            pltpu.VMEM((n, planes * hid, chunk), BF),
            pltpu.VMEM((n, planes * hid, chunk), BF),
            pltpu.VMEM((n, planes * chans, chunk), BF),
            pltpu.VMEM((n, planes, chunk), F32),
            pltpu.VMEM((n, planes, chunk), F32),
            pltpu.VMEM((n, planes, chunk), F32),
            pltpu.VMEM((halves, rows, chunk), BF),
            pltpu.VMEM((PACK * hid, PACK * feats), BF),
            pltpu.VMEM((PACK * feats, PACK * hid), BF),
            pltpu.VMEM((halves, rows, PACK * hid), BF),
            pltpu.VMEM((halves, PACK * hid, rows), BF),
            pltpu.VMEM((PACK * hid, PACK * feats), F32),
            pltpu.VMEM((halves, rows, PACK * hid), F32),
            pltpu.VMEM((n, chans, chunk), BF),
            pltpu.VMEM((n, chans, chunk), BF),
            pltpu.VMEM((n, chans, chunk), BF),
            pltpu.VMEM((n, 1, chunk), F32),
            pltpu.VMEM((n, 1, chunk), F32),
            pltpu.VMEM((n, 2, chunk), F32),
            pltpu.VMEM((n, 2, chunk), F32),
            pltpu.VMEM((8, chunk), F32),
            pltpu.VMEM((planes, chunk), F32),
            pltpu.VMEM(part, F32),
            pltpu.VMEM(part, F32),
            pltpu.VMEM(part[1:], F32),
            pltpu.VMEM(part, F32),
        ]
        + [dma((n,))] * 6
        + [dma((n // 2,)), dma((n,)), dma((n,))]
        + [dma((n,))] * 4,
        compiler_params=pltpu.CompilerParams(
            vmem_limit_bytes=LIMIT, collective_id=1, has_side_effects=True
        ),
        name="fused",
    )(pltpu.with_memory_space_constraint(sheared, pltpu.VMEM), w_first.T, w_second, cotangent)
    gvox, image, g1, g2 = pl.pallas_call(
        place_kernel,
        out_shape=(jax.ShapeDtypeStruct(voxels.shape, BF),) + small,
        in_specs=[smem] + [vmem] * 4,
        out_specs=(hbm, vmem, vmem, vmem),
        scratch_shapes=[dma],
        compiler_params=pltpu.CompilerParams(vmem_limit_bytes=4 * 2**20),
        name="place",
    )(offsets, *(pltpu.with_memory_space_constraint(a, pltpu.VMEM) for a in (gsh, image, g1, g2)))
    return image, gvox, g1.T, g2


def solution(mesh):
    placed = (
        P(("groups", "depth"), None, None),
        P("groups"),
        P(),
        P(),
        P(None, ("groups", "depth")),
    )
    return jax.shard_map(
        shards,
        mesh=mesh,
        in_specs=placed,
        out_specs=(
            P(None, ("groups", "depth")),
            P(("groups", "depth"), None, None),
            P("groups", None),
            P("groups", None),
        ),
        check_vma=False,
    )
```

```python
import functools

import jax
import jax.numpy as jnp
from jax import lax
from jax.experimental import pallas as pl
from jax.experimental.pallas import tpu as pltpu
from jax.sharding import PartitionSpec as P

TILE = 128
PACK = 4
FSUB = 1024
BSUB = 256
GSUB = 512
CSUB = 512
LIMIT = 190 * 2**18
BF = jnp.bfloat16
F32 = jnp.float32
NT = (((1,), (1,)), ((), ()))


def dot(a, b):
    return jnp.dot(a, b, preferred_element_type=F32)


def running_sum(x):
    rows = x.shape[0]
    row = lax.broadcasted_iota(jnp.int32, x.shape, 0)
    s = 1
    while s < rows:
        x = x + jnp.where(row >= s, pltpu.roll(x, s, 0), 0.0)
        s *= 2
    return x


def wrap(t, total):
    if total & (total - 1) == 0:
        return t & (total - 1)
    return lax.rem(t, total)


def first_tile(off_ref, planes, p):
    return off_ref[lax.axis_index("depth") * planes + p]


def tile_at(base, j, rays):
    return pl.ds(pl.multiple_of(wrap(base + j, rays // TILE) * TILE, TILE), TILE)


def absorb(dens):
    upto = running_sum(dens)
    passing = jnp.exp(-dens)
    before = jnp.exp(dens - upto)
    return upto, passing, before


def softplus(x):
    return jnp.maximum(x, 0.0) + jnp.log1p(jnp.exp(-jnp.abs(x)))


def picks(shape, period, dim):
    other = lax.broadcasted_iota(jnp.int32, shape, 1 - dim)
    return (lax.rem(lax.broadcasted_iota(jnp.int32, shape, dim), period) == other).astype(BF)


def diagonal(shape, rows, cols):
    r = lax.broadcasted_iota(jnp.int32, shape, 0) // rows
    return r == lax.broadcasted_iota(jnp.int32, shape, 1) // cols


def repeat_blocks(w):
    rows, cols = w.shape
    tall = dot(picks((PACK * rows, rows), rows, 0), w).astype(BF)
    full = dot(tall, picks((cols, PACK * cols), cols, 1))
    return jnp.where(diagonal(full.shape, rows, cols), full, 0.0)


def prepare(first_ref, second_ref, w1_ref, w1t_ref, w2_ref, w2t_ref):
    planes = PACK * w2_ref.shape[0]
    chans, hid = second_ref.shape[0] - 1, second_ref.shape[1]
    w1t = repeat_blocks(first_ref[...])
    w1t_ref[...] = w1t.astype(BF)
    w1_ref[...] = (0.5 * w1t).T.astype(BF)
    rad = repeat_blocks(second_ref[0:chans, :])
    dens = dot(second_ref[chans : chans + 1, :], picks((hid, PACK * hid), hid, 1))
    dens = jnp.broadcast_to(dens, (planes, PACK * hid))
    block = lax.broadcasted_iota(jnp.int32, dens.shape, 1) // hid
    plane = lax.broadcasted_iota(jnp.int32, dens.shape, 0)
    for h in range(planes // PACK):
        mine = jnp.where(plane == block + h * PACK, dens, 0.0)
        w2_ref[h] = jnp.concatenate([0.5 * rad, mine], 0).astype(BF)
        w2t_ref[h] = (0.5 * jnp.concatenate([rad, mine], 0)).T.astype(BF)


def remote(src, dst, send_sem, recv_sem, to):
    return pltpu.make_async_remote_copy(
        src_ref=src,
        dst_ref=dst,
        send_sem=send_sem,
        recv_sem=recv_sem,
        device_id={"depth": to},
        device_id_type=pl.DeviceIdType.MESH,
    )


def turn(i, n):
    if n & (n - 1):
        return i
    c, bit = 0, 1
    while bit < n:
        c = c + ((i // bit) % 2) * (n // (2 * bit))
        bit *= 2
    return c


def each(n, body):
    def step(d, carry):
        body(d)
        return carry

    lax.fori_loop(0, n, step, 0)


def fused_kernel(
    dscale,
    xs,
    first_ref,
    second_ref,
    cot_ref,
    image_ref,
    gsh,
    g1_ref,
    g2_ref,
    hids,
    slope,
    srad,
    wgt,
    bpass,
    dsig,
    graw,
    w1,
    w1t,
    w2,
    w2t,
    acc1,
    acc2,
    cots,
    csend,
    crecv,
    tsend,
    trecv,
    back,
    land,
    held,
    raw_ref,
    give,
    got,
    mine,
    full,
    sem_c,
    rem_c,
    sem_t,
    rem_t,
    sem_b,
    rem_b,
    sem_k,
    rem_k,
    sem_r,
    s1,
    r1,
    s2,
    r2,
):
    n, chans, width = cots.shape
    halves, rows = w2.shape[0], w2.shape[1]
    planes = PACK * halves
    feats = xs.shape[1] // planes
    kin, kmid = w1.shape[1], w1.shape[0]
    wide = rows - planes
    me = lax.axis_index("depth")
    chip, core = me // 2, me % 2
    partner = me + 1 - 2 * core

    barrier = pltpu.get_barrier_semaphore()
    for s in range(1, n):
        pl.semaphore_signal(
            barrier,
            inc=1,
            device_id={"depth": (me + s) % n},
            device_id_type=pl.DeviceIdType.MESH,
        )
    cots[me] = cot_ref[...].astype(BF)
    acc1[...] = jnp.zeros_like(acc1)
    acc2[...] = jnp.zeros_like(acc2)
    prepare(first_ref, second_ref, w1, w1t, w2, w2t)
    pl.semaphore_wait(barrier, n - 1)

    def colour_copy(c):
        return remote(csend.at[c], crecv.at[me], sem_c.at[c], rem_c.at[me], c)

    def colour_here(d):
        return remote(csend.at[d], crecv.at[d], sem_c.at[d], rem_c.at[d], d)

    def through_copy(c):
        return remote(tsend.at[c], trecv.at[me], sem_t.at[c], rem_t.at[me], c)

    def through_here(d):
        return remote(tsend.at[d], trecv.at[d], sem_t.at[d], rem_t.at[d], d)

    def reply_copy(d):
        return remote(back.at[d], land.at[me], sem_b.at[d], rem_b.at[me], d)

    def reply_here(c):
        return remote(back.at[c], land.at[c], sem_b.at[c], rem_b.at[c], c)

    def cot_copy(s):
        to = partner if s == 0 else (me + 2 * s) % n
        return remote(cots.at[me], cots.at[me], sem_k.at[s], rem_k.at[me], to)

    def relay_copy(c):
        return remote(cots.at[c], cots.at[c], sem_r.at[c], rem_k.at[c], partner)

    def relays(c):
        return jnp.logical_and(c % 2 == core, c != me)

    def give_cot(c):
        @pl.when(c == me)
        def _():
            for s in range(n // 2):
                cot_copy(s).start()

    def pass_cot(c):
        @pl.when(relays(c))
        def _():
            relay_copy(c).wait_recv()
            relay_copy(c).start()

    def weigh(c):
        @pl.when(c % 2 != core)
        def _():
            relay_copy(c).wait_recv()

        worth = cots[c].astype(F32) * csend[c].astype(F32)
        tsend[c, 1:2, :] = jnp.sum(worth, axis=0, keepdims=True)

    def hand_on(c):
        @pl.when(c != me)
        def _():
            through_copy(c).start()

        @pl.when(c == me)
        def _():
            trecv[me] = tsend[me]

    def give_colour(c):
        @pl.when(c != me)
        def _():
            colour_copy(c).start()

    def settle(c):
        @pl.when(c == me)
        def _():
            def arrived(d):
                @pl.when(d != me)
                def _():
                    through_here(d).wait_recv()

            each(n, arrived)
            row = lax.broadcasted_iota(jnp.int32, held.shape, 0)
            held[...] = (row == 0).astype(F32)

            def fold(d):
                enter = held[0:1, :]
                prior = held[1:2, :]
                back[d, 0:1, :] = enter
                back[d, 1:2, :] = prior
                held[2:4, :] = trecv[d]
                held[1:2, :] = prior + enter * held[3:4, :]
                held[0:1, :] = enter * held[2:3, :]

            each(n, fold)
            total = held[1:2, :]

            def turn_round(d):
                back[d, 1:2, :] = total - back[d, 1:2, :]

            each(n, turn_round)

            def answer(d):
                @pl.when(d != me)
                def _():
                    reply_copy(d).start()

            each(n, answer)
            land[me] = back[me]

    duties = (
        (n // 2 - 2, pass_cot),
        (n // 2 + 1, weigh),
        (n // 2 + 2, hand_on),
        (n - 4, give_colour),
        (n - 3, settle),
    )

    def serve(step, lags):
        for lag, duty in lags:

            @pl.when(jnp.logical_and(step >= lag, step < lag + n))
            def _():
                duty(turn(step - lag, n))

    fsub = min(FSUB, width)
    csub = min(CSUB, width)
    stack = picks((chans, planes * chans), chans, 1)

    def forward(i, carry):
        c = turn(i, n)

        @pl.when(i < n // 2)
        def _():
            give_cot(turn(2 * i, n))
            give_cot(turn(2 * i + 1, n))

        serve(i, duties)

        for b in range(width // fsub):
            here = pl.ds(b * fsub, fsub)
            raw_d = None
            for h in range(halves):
                mid = pl.ds(h * kmid, kmid)
                half = dot(w1[...], xs[c, pl.ds(h * kin, kin), here]).astype(BF)
                t = jnp.tanh(half)
                up = 1.0 + t
                hidden = half * up
                slope[c, mid, here] = up + hidden * (1.0 - t)
                hids[c, mid, here] = hidden
                out = dot(w2[h], hidden)
                srad[c, pl.ds(h * wide, wide), here] = jnp.tanh(out[:wide].astype(BF))
                d = out[wide:]
                raw_d = d if raw_d is None else raw_d + d
            raw_ref[:, here] = raw_d
        raw_d = raw_ref[...]
        dens = softplus(raw_d) * dscale
        upto, passing, before = absorb(dens)
        weight = before * (1.0 - passing)
        wgt[c] = weight
        bpass[c] = before * passing
        dsig[c] = dscale * (0.5 * jnp.tanh(0.5 * raw_d) + 0.5)
        weight = 0.5 * weight
        tsend[c, 0:1, :] = jnp.exp(-upto[planes - 1 : planes])
        plain = jnp.sum(weight, axis=0, keepdims=True)
        for b in range(width // csub):
            at = slice(b * csub, (b + 1) * csub)
            here = pl.ds(b * csub, csub)
            shares = []
            for p in range(planes):
                w = jnp.broadcast_to(weight[p : p + 1, at], (chans, csub)).astype(BF)
                shares.append(w * srad[c, pl.ds(p * chans, chans), here])
            colour = plain[:, at] + dot(stack, jnp.concatenate(shares, 0))
            csend[c, :, here] = colour.astype(BF)
        return carry

    lax.fori_loop(0, n, forward, 0)

    ones = diagonal((planes, planes * chans), 1, chans).astype(BF)
    bsub = min(BSUB, width)

    def backward(i, carry):
        c = turn(i, n)

        serve(i + n, duties)

        @pl.when(c != me)
        def _():
            reply_here(c).wait_recv()

        for b in range(width // csub):
            here = pl.ds(b * csub, csub)
            cot = cots[c, :, here]
            prod = jnp.concatenate(
                [cot * srad[c, pl.ds(p * chans, chans), here] for p in range(planes)], 0
            )
            raw_ref[:, here] = dot(ones, prod)
        score = 0.5 * (jnp.sum(cots[c].astype(F32), axis=0, keepdims=True) + raw_ref[...])
        enter = land[c, 0:1, :]
        rest = land[c, 1:2, :]
        weight = enter * wgt[c]
        running = running_sum(weight * score)
        grad_d = enter * bpass[c] * score - (rest - running)
        grad_d = (grad_d * dsig[c]).astype(BF)
        weight = 0.25 * weight
        for h in range(halves):
            graw[h, pl.ds(wide, planes), :] = grad_d
        for b in range(width // bsub):
            at = slice(b * bsub, (b + 1) * bsub)
            here = pl.ds(b * bsub, bsub)
            cot = cots[c, :, here]
            for h in range(halves):
                for k in range(PACK):
                    p = h * PACK + k
                    s = srad[c, pl.ds(p * chans, chans), here]
                    w = jnp.broadcast_to(weight[p : p + 1, at], (chans, bsub)).astype(BF)
                    graw[h, pl.ds(k * chans, chans), here] = (w * cot) * (1.0 - s * s)
                ghid = dot(w2t[h], graw[h, :, here]).astype(BF)
                mid = pl.ds(h * kmid, kmid)
                slope[c, mid, here] = ghid * slope[c, mid, here]
        for h in range(halves):
            mid = pl.ds(h * kmid, kmid)
            acc1[...] += lax.dot_general(
                slope[c, mid, :], xs[c, pl.ds(h * kin, kin), :], NT, preferred_element_type=F32
            )
            acc2[h] += lax.dot_general(graw[h], hids[c, mid, :], NT, preferred_element_type=F32)
        return carry

    lax.fori_loop(0, n, backward, 0)

    fold_grads(n, acc1, acc2, feats, chans, give)
    copies = swap(n, me, lambda to: give.at[to], got, s1, r1)
    got[me] = give[me]

    gsub = min(GSUB, width)

    def voxel_grads(c, carry):
        for b in range(width // gsub):
            here = pl.ds(b * gsub, gsub)
            for h in range(halves):
                gx = dot(w1t[...], slope[c, pl.ds(h * kmid, kmid), here])
                gsh[c, pl.ds(h * kin, kin), here] = gx.astype(BF)
        return carry

    lax.fori_loop(0, n // 2, voxel_grads, 0)
    for copy in copies:
        copy.wait()
    mine[...] = jnp.sum(got[...], axis=0)
    copies = swap(n, me, lambda to: mine, full, s2, r2)
    full[me] = mine[...]
    lax.fori_loop(n // 2, n, voxel_grads, 0)
    image_ref[...] = back[me, 0:1, :] * csend[me].astype(F32)

    def add_colour(d):
        @pl.when(d != me)
        def _():
            colour_here(d).wait_recv()
            image_ref[...] += back[d, 0:1, :] * crecv[d].astype(F32)

    each(n, add_colour)
    for copy in copies:
        copy.wait()
    both = jnp.concatenate([full[d] for d in range(n)], 0)
    g2_ref[...] = both[: chans + 1, : both.shape[0]]
    square = jnp.concatenate([both, jnp.zeros_like(both)], 0).T
    g1_ref[...] = square[both.shape[0] : both.shape[0] + feats, : both.shape[0]]

    def finish(d):
        @pl.when(d != me)
        def _():
            colour_copy(d).wait_send()
            through_copy(d).wait_send()
            reply_copy(d).wait_send()

        @pl.when(relays(d))
        def _():
            relay_copy(d).wait_send()

    each(n, finish)
    for s in range(n // 2):
        cot_copy(s).wait_send()


def swap(n, me, source, target, send_sem, recv_sem):
    copies = []
    for s in range(1, n):
        to = lax.rem(me + s, n)
        copies.append(remote(source(to), target.at[me], send_sem.at[s], recv_sem.at[s], to))
    for copy in copies:
        copy.start()
    return copies


def whole_tiles(x):
    short = -x.shape[1] % TILE
    return jnp.concatenate([x, jnp.zeros((x.shape[0], short), x.dtype)], 1) if short else x


def fold_grads(n, a1_ref, a2_ref, feats, chans, give):
    hid = a1_ref.shape[0] // PACK
    halves, rows = a2_ref.shape[0], a2_ref.shape[1]
    part = give.shape[1]

    def aligned(ref_rows, k, size):
        at = k * size
        lane = at % TILE
        piece = ref_rows[:, at - lane : at - lane + TILE]
        return pltpu.roll(piece, TILE - lane, 1) if lane else piece

    g1 = g2 = gd = None
    for k in range(PACK):
        one = aligned(whole_tiles(a1_ref[pl.ds(k * hid, hid), :]), k, feats)
        g1 = one if g1 is None else g1 + one
    for h in range(halves):
        tail = a2_ref[h, pl.ds(PACK * chans, rows - PACK * chans), :]
        row = lax.broadcasted_iota(jnp.int32, (tail.shape[0], TILE), 0)
        for k in range(PACK):
            two = aligned(a2_ref[h, pl.ds(k * chans, chans), :], k, hid)
            g2 = two if g2 is None else g2 + two
            dens = jnp.where(row == h * PACK + k, aligned(tail, k, hid), 0.0)
            dens = jnp.sum(dens, axis=0, keepdims=True)
            gd = dens if gd is None else gd + dens
    lanes = lax.broadcasted_iota(jnp.int32, (hid, TILE), 1)
    rest = hid - chans - 1
    low = jnp.concatenate([g2, gd, jnp.zeros((rest, TILE), F32)], 0)
    both = jnp.where(lanes < hid, low, pltpu.roll(g1, hid, 1))
    for d in range(n):
        give[d] = both[d * part : (d + 1) * part]


def moves(off_ref, planes, feats, n, width, rays, pair):
    me = lax.axis_index("depth")
    tiles, per = rays // TILE, width // TILE
    for p in range(planes):
        base = off_ref[me * planes + p]
        rows = pl.ds(p * feats, feats)

        def chunk(c):
            first = wrap(base + c * per, tiles)

            @pl.when(first + per <= tiles)
            def _():
                at = pl.ds(pl.multiple_of(first * TILE, TILE), width)
                pair((p, slice(None), at), (c, rows)).start()

            @pl.when(first + per > tiles)
            def _():
                for j in range(per):
                    spot = (c, rows, pl.ds(j * TILE, TILE))
                    pair((p, slice(None), tile_at(first, j, rays)), spot).start()

        each(n, chunk)


def shear_kernel(off_ref, vox_ref, x_ref, sem):
    planes, feats, rays = vox_ref.shape
    n, _, width = x_ref.shape

    def pair(plain, sheared):
        return pltpu.make_async_copy(vox_ref.at[plain], x_ref.at[sheared], sem)

    moves(off_ref, planes, feats, n, width, rays, pair)
    pltpu.make_async_copy(x_ref, x_ref, sem).wait()


def place_kernel(off_ref, gsh_ref, image_in, g1_in, g2_in, gvox_ref, image_ref, g1_ref, g2_ref, sem):
    planes, feats, rays = gvox_ref.shape
    n, _, width = gsh_ref.shape

    def pair(plain, sheared):
        return pltpu.make_async_copy(gsh_ref.at[sheared], gvox_ref.at[plain], sem)

    moves(off_ref, planes, feats, n, width, rays, pair)
    image_ref[...] = image_in[...]
    g1_ref[...] = g1_in[...]
    g2_ref[...] = g2_in[...]
    pltpu.make_async_copy(gsh_ref, gsh_ref, sem).wait()


def shards(voxels, offsets, w_first, w_second, cotangent):
    planes, feats, rays = voxels.shape
    hid = w_first.shape[0]
    chans, chunk = cotangent.shape
    n = lax.axis_size("depth")
    halves = planes // PACK
    dscale = 3.0 / (planes * n)
    rows = PACK * chans + planes

    smem = pl.BlockSpec(memory_space=pltpu.SMEM)
    vmem = pl.BlockSpec(memory_space=pltpu.VMEM)
    hbm = pl.BlockSpec(memory_space=pltpu.HBM)
    small = (
        jax.ShapeDtypeStruct((chans, chunk), F32),
        jax.ShapeDtypeStruct((feats, hid), F32),
        jax.ShapeDtypeStruct((chans + 1, hid), F32),
    )
    held = tuple(pltpu.VMEM(a.shape, F32) for a in small)
    part = (n, hid // n, TILE)
    dma = pltpu.SemaphoreType.DMA
    chunks = pltpu.VMEM((n, planes * feats, chunk), BF)
    sheared = pl.pallas_call(
        shear_kernel,
        out_shape=chunks,
        in_specs=[smem, hbm],
        out_specs=vmem,
        scratch_shapes=[dma],
        compiler_params=pltpu.CompilerParams(vmem_limit_bytes=4 * 2**20),
        name="shear",
    )(offsets, pltpu.with_memory_space_constraint(voxels, pltpu.HBM))
    image, gsh, g1, g2 = pl.pallas_call(
        functools.partial(fused_kernel, dscale),
        out_shape=(held[0], chunks) + held[1:],
        in_specs=[vmem, vmem, vmem, vmem],
        out_specs=(vmem, vmem, vmem, vmem),
        scratch_shapes=[
            pltpu.VMEM((n, planes * hid, chunk), BF),
            pltpu.VMEM((n, planes * hid, chunk), BF),
            pltpu.VMEM((n, planes * chans, chunk), BF),
            pltpu.VMEM((n, planes, chunk), F32),
            pltpu.VMEM((n, planes, chunk), F32),
            pltpu.VMEM((n, planes, chunk), F32),
            pltpu.VMEM((halves, rows, chunk), BF),
            pltpu.VMEM((PACK * hid, PACK * feats), BF),
            pltpu.VMEM((PACK * feats, PACK * hid), BF),
            pltpu.VMEM((halves, rows, PACK * hid), BF),
            pltpu.VMEM((halves, PACK * hid, rows), BF),
            pltpu.VMEM((PACK * hid, PACK * feats), F32),
            pltpu.VMEM((halves, rows, PACK * hid), F32),
            pltpu.VMEM((n, chans, chunk), BF),
            pltpu.VMEM((n, chans, chunk), BF),
            pltpu.VMEM((n, chans, chunk), BF),
            pltpu.VMEM((n, 2, chunk), F32),
            pltpu.VMEM((n, 2, chunk), F32),
            pltpu.VMEM((n, 2, chunk), F32),
            pltpu.VMEM((n, 2, chunk), F32),
            pltpu.VMEM((8, chunk), F32),
            pltpu.VMEM((planes, chunk), F32),
            pltpu.VMEM(part, F32),
            pltpu.VMEM(part, F32),
            pltpu.VMEM(part[1:], F32),
            pltpu.VMEM(part, F32),
        ]
        + [dma((n,))] * 6
        + [dma((n // 2,)), dma((n,)), dma((n,))]
        + [dma((n,))] * 4,
        compiler_params=pltpu.CompilerParams(
            vmem_limit_bytes=LIMIT, collective_id=1, has_side_effects=True
        ),
        name="fused",
    )(pltpu.with_memory_space_constraint(sheared, pltpu.VMEM), w_first.T, w_second, cotangent)
    gvox, image, g1, g2 = pl.pallas_call(
        place_kernel,
        out_shape=(jax.ShapeDtypeStruct(voxels.shape, BF),) + small,
        in_specs=[smem] + [vmem] * 4,
        out_specs=(hbm, vmem, vmem, vmem),
        scratch_shapes=[dma],
        compiler_params=pltpu.CompilerParams(vmem_limit_bytes=4 * 2**20),
        name="place",
    )(offsets, *(pltpu.with_memory_space_constraint(a, pltpu.VMEM) for a in (gsh, image, g1, g2)))
    return image, gvox, g1.T, g2


def solution(mesh):
    placed = (
        P(("groups", "depth"), None, None),
        P("groups"),
        P(),
        P(),
        P(None, ("groups", "depth")),
    )
    return jax.shard_map(
        shards,
        mesh=mesh,
        in_specs=placed,
        out_specs=(
            P(None, ("groups", "depth")),
            P(("groups", "depth"), None, None),
            P("groups", None),
            P("groups", None),
        ),
        check_vma=False,
    )
```
